32 devices in a mesh: mz: 8 (over z, x), rep: 4 (over y, core).
Axes of the slice: x: 2, y: 2, z: 4, core: 2. Of those that a mesh axis runs over, the one named last changes fastest.
Arguments:
- spectra: bfloat16 [131072, 512], P(('mz', 'rep')), may hold values from -6 to 6
- reach_back: int32 [131072], P(('mz', 'rep')), may hold values from 0 to 256
- reach_ahead: int32 [131072], P(('mz', 'rep')), may hold values from 0 to 256
- live: int32 [32], P(('mz', 'rep')), may hold values from 1024 to 4096, as said below
- cluster_ids: int32 [131072], P(('mz', 'rep')), may hold values from 0 to 16383, as said below
Outputs:
- cluster_vectors: float32 [16384, 512], P(('mz', 'rep'))
The draws below stay inside these ranges and needn't reach their ends.
Inputs may be any that keep to these rules, and one draw needn't show every extreme that they name: Device d holds slots d * 4096 to (d + 1) * 4096 - 1, of which the first live[d] are occupied; at least one device is full. `cluster_ids`: cluster k is owned by m/z range k div (512 * 4). Range d is held by devices d * 4 to d * 4 + 4 - 1 in order of rising m/z; a spectrum on the first of them belongs to a cluster owned by range d - 1 or d, one on the last of them to a cluster owned by range d or d + 1, and one on any other to a cluster owned by range d.
All inputs are finite; a program needn't handle non-finite values.
Results may differ from the reference program's by a relative error of at most 0.0046.
Values may be sent and summed in bfloat16 or wider, within the bound.
A program may use at most 128 MiB of HBM per device.

```python
import jax
import jax.numpy as jnp
from jax import lax

DIM = 512
BLOCK = 256
ROWS_DEV = 4096
CL_DEV = 512
NSPEC = 131072
NCLUST = 16384
N_MZ = 8
N_REP = 4


def draw_live(key, part):
    count = N_MZ * N_REP
    values = jax.random.randint(key, (count,), ROWS_DEV // 4, ROWS_DEV + 1)
    full = jax.random.randint(jax.random.fold_in(key, 7), (), 0, count)
    return jnp.where(jnp.arange(count) == full, ROWS_DEV, values).astype(jnp.int32)


def draw_cluster_ids(key, part):
    total_rows = ROWS_DEV * N_MZ * N_REP
    position = jnp.arange(total_rows, dtype=jnp.int32)
    range_index = position // (ROWS_DEV * N_REP)
    rep_index = position // ROWS_DEV % N_REP
    coin = jax.random.randint(jax.random.fold_in(key, 3), (total_rows,), 0, 4)
    away = coin != 0
    step = jnp.where((rep_index == 0) & away, -1, jnp.where((rep_index == N_REP - 1) & away, 1, 0))
    owner = jnp.clip(range_index + step, 0, N_MZ - 1)
    inner = jax.random.randint(jax.random.fold_in(key, 5), (total_rows,), 0, CL_DEV * N_REP)
    return (owner * (CL_DEV * N_REP) + inner).astype(jnp.int32)


def plant(result, key, low, largest):
    shape = result.shape
    spot = [jax.random.randint(jax.random.fold_in(key, axis), (), 0, shape[axis]) for axis in range(len(shape))]
    result = result.at[tuple(spot)].set(low)
    longest = shape.index(max(shape))
    spot[longest] = (spot[longest] + 1) % shape[longest]
    return result.at[tuple(spot)].set(largest)


def block_scale(stream_key, shape, cuts, least, high):
    gain, own = 1.0, jax.random.fold_in(stream_key, 6)
    for dim, parts in cuts:
        draws = jnp.exp(jax.random.uniform(jax.random.fold_in(own, dim), (parts,), jnp.float32, least / len(cuts), high / len(cuts)))
        gain = gain * jnp.repeat(draws, shape[dim] // parts).reshape([-1 if axis == dim else 1 for axis in range(len(shape))])
    return gain


def centred(stream_key, shape, scale, bound, cuts=(), held_as=jnp.bfloat16):
    level = block_scale(stream_key, shape, cuts, -0.22, 0.18) if cuts else 1.0
    array = jax.random.normal(stream_key, shape, jnp.float32) * scale * level
    return jnp.minimum(jnp.maximum(array, -bound), bound).astype(held_as)


def setup_inputs(seed: int = 0) -> dict:
    key_list = jax.random.split(jax.random.key(seed), 6)
    return {
        "spectra": centred(key_list[0], (NSPEC, DIM), 1.0, 6.0, ((0, 32),)),
        "reach_back": plant(jax.random.randint(key_list[1], (NSPEC,), 0, BLOCK + 1), jax.random.fold_in(key_list[1], 1), 0, BLOCK).astype(jnp.int32),
        "reach_ahead": plant(jax.random.randint(key_list[2], (NSPEC,), 0, BLOCK + 1), jax.random.fold_in(key_list[2], 1), 0, BLOCK).astype(jnp.int32),
        "live": draw_live(jax.random.fold_in(key_list[5], 71), 0),
        "cluster_ids": draw_cluster_ids(jax.random.fold_in(key_list[5], 71), 0),
    }


sharpness = 3.0

def rows_block(queries, query_pos, back, ahead, keys, key_flags, key_start):
    scores = lax.dot_general(queries, keys, (((1,), (1,)), ((), ())), preferred_element_type=jnp.float32)
    key_pos = key_start + jnp.arange(keys.shape[0], dtype=jnp.int32)
    offset = key_pos[None, :] - query_pos[:, None]
    inside = (offset >= -back[:, None]) & (offset <= ahead[:, None]) & (key_flags[None, :] > 0)
    keep = inside | (offset == 0)
    weight = jnp.where(keep, jnp.exp(sharpness * (scores - 1.0)), jnp.float32(0.0))
    total = lax.optimization_barrier(jnp.sum(weight, axis=1, keepdims=True))
    mixed = jnp.dot(weight.astype(jnp.bfloat16), keys, preferred_element_type=jnp.float32)
    return (mixed / total).astype(jnp.bfloat16)

def reference(spectra, reach_back, reach_ahead, live, cluster_ids):
    total_rows = spectra.shape[0]
    values = spectra.astype(jnp.float32)
    unit = (values / jnp.sqrt(lax.optimization_barrier(jnp.sum(values * values, axis=1, keepdims=True)) + 1e-06)).astype(jnp.bfloat16)
    position = jnp.arange(total_rows, dtype=jnp.int32)
    present = position % ROWS_DEV < live[position // ROWS_DEV]
    flags = present.astype(jnp.bfloat16)
    padded_unit = jnp.pad(unit, ((BLOCK, BLOCK), (0, 0)))
    padded_flags = jnp.pad(flags, (BLOCK, BLOCK))

    def one_block(index):
        start = (index * BLOCK).astype(jnp.int32)
        queries = lax.dynamic_slice_in_dim(unit, start, BLOCK, 0)
        back = lax.dynamic_slice_in_dim(reach_back, start, BLOCK, 0)
        ahead = lax.dynamic_slice_in_dim(reach_ahead, start, BLOCK, 0)
        keys = lax.dynamic_slice_in_dim(padded_unit, start, 3 * BLOCK, 0)
        key_flags = lax.dynamic_slice_in_dim(padded_flags, start, 3 * BLOCK, 0)
        query_pos = start + jnp.arange(BLOCK, dtype=jnp.int32)
        return rows_block(queries, query_pos, back, ahead, keys, key_flags, start - BLOCK)
    blocks = lax.map(one_block, jnp.arange(total_rows // BLOCK, dtype=jnp.int32))
    consensus = blocks.reshape(total_rows, DIM)
    kept = consensus.astype(jnp.float32) * present.astype(jnp.float32)[:, None]
    sums = jax.ops.segment_sum(kept, cluster_ids, num_segments=NCLUST)
    scale = jnp.sqrt(lax.optimization_barrier(jnp.mean(sums * sums, axis=1, keepdims=True)) + 1e-06)
    return sums / scale
```

```python
import jax
import jax.numpy as jnp
from jax import lax
from jax.sharding import PartitionSpec as P

DIM = 512
BLOCK = 256
CL_DEV = 512


sharpness = 3.0


def extended(block, sides, width):
    for axis, dim in sides:
        count = lax.axis_size(axis)
        forward = [(i, i + 1) for i in range(count - 1)]
        backward = [(target, source) for source, target in forward]
        low = lax.ppermute(
            lax.slice_in_dim(block, block.shape[dim] - width, None, axis=dim), axis, forward
        )
        high = lax.ppermute(lax.slice_in_dim(block, 0, width, axis=dim), axis, backward)
        block = jnp.concatenate([low, block, high], axis=dim)
    return block


def shifted(block, axis, distance):
    devices = range(lax.axis_size(axis))
    route = [(i - distance, i) for i in devices if i - distance in devices]
    return lax.ppermute(block, axis, route)


def rows_block(queries, query_pos, back, ahead, keys, key_flags, key_start):
    scores = lax.dot_general(
        queries, keys, (((1,), (1,)), ((), ())), preferred_element_type=jnp.float32
    )
    key_pos = key_start + jnp.arange(keys.shape[0], dtype=jnp.int32)
    offset = key_pos[None, :] - query_pos[:, None]
    inside = (offset >= -back[:, None]) & (offset <= ahead[:, None]) & (key_flags[None, :] > 0)
    keep = inside | (offset == 0)
    weight = jnp.where(keep, jnp.exp(sharpness * (scores - 1.0)), jnp.float32(0.0))
    total = jnp.sum(weight, axis=1, keepdims=True)
    mixed = jnp.dot(weight.astype(jnp.bfloat16), keys, preferred_element_type=jnp.float32)
    return (mixed / total).astype(jnp.bfloat16)


def shards(spectra, reach_back, reach_ahead, live, cluster_ids):
    rows = spectra.shape[0]
    values = spectra.astype(jnp.float32)
    unit = (values / jnp.sqrt(jnp.sum(values * values, axis=1, keepdims=True) + 1e-06)).astype(
        jnp.bfloat16
    )
    present = jnp.arange(rows, dtype=jnp.int32) < live[0]
    flags = present.astype(jnp.bfloat16)
    wide_unit, wide_flags = (
        extended(unit, ((("mz", "rep"), 0),), BLOCK),
        extended(flags, ((("mz", "rep"), 0),), BLOCK),
    )
    pieces = []
    for index in range(rows // BLOCK):
        start = index * BLOCK
        query_pos = start + jnp.arange(BLOCK, dtype=jnp.int32)
        pieces.append(
            rows_block(
                unit[start : start + BLOCK],
                query_pos,
                reach_back[start : start + BLOCK],
                reach_ahead[start : start + BLOCK],
                wide_unit[start : start + 3 * BLOCK],
                wide_flags[start : start + 3 * BLOCK],
                start - BLOCK,
            )
        )
    consensus = jnp.concatenate(pieces, axis=0)
    kept = consensus.astype(jnp.float32) * present.astype(jnp.float32)[:, None]
    rep_count = lax.axis_size("rep")
    per_range = CL_DEV * rep_count
    span = 2 * per_range
    local = cluster_ids - lax.axis_index("mz") * per_range
    slot = jnp.where(local < 0, local + span, local)
    partial_value = jax.ops.segment_sum(kept, slot, num_segments=span).astype(jnp.bfloat16)
    parts = partial_value.reshape(2, rep_count, CL_DEV, DIM)
    arrived = lax.all_to_all(parts[0], "rep", split_axis=0, concat_axis=0, tiled=True)
    owned = jnp.sum(arrived.astype(jnp.float32), axis=0)
    mz_count = lax.axis_size("mz")
    first = lax.axis_index("rep") == 0
    turn = rep_count // 2
    for step in range(rep_count):
        other = (step + turn) % rep_count
        route = [(d * rep_count, (d - 1) * rep_count + step) for d in range(1, mz_count)]
        route += [
            (d * rep_count + rep_count - 1, (d + 1) * rep_count + other)
            for d in range(mz_count - 1)
        ]
        piece = jnp.where(first, parts[1, step], parts[1, other])
        owned = owned + lax.ppermute(piece, ("mz", "rep"), route).astype(jnp.float32)
    scale = jnp.sqrt(jnp.mean(owned * owned, axis=1, keepdims=True) + 1e-06)
    return owned / scale


def solution(mesh):
    return jax.shard_map(
        shards,
        mesh=mesh,
        in_specs=(
            P(("mz", "rep"), None),
            P(("mz", "rep")),
            P(("mz", "rep")),
            P(("mz", "rep")),
            P(("mz", "rep")),
        ),
        out_specs=P(("mz", "rep"), None),
        check_vma=False,
    )
```

```python
import functools

import jax
import jax.numpy as jnp
from jax import lax
from jax.experimental import pallas as pl
from jax.experimental.pallas import tpu as pltpu
from jax.sharding import PartitionSpec as P

BLOCK = 256
CL_DEV = 512
TILE = 256
MESH = pl.DeviceIdType.MESH

sharpness = 3.0


def remote(src, dst, send_sem, recv_sem, device):
    return pltpu.make_async_remote_copy(
        src_ref=src,
        dst_ref=dst,
        send_sem=send_sem,
        recv_sem=recv_sem,
        device_id=device,
        device_id_type=MESH,
    )


def kernel(
    M,
    R,
    x_hbm,
    reach_ref,
    live_ref,
    ids_ref,
    out_ref,
    raw,
    ext,
    cons,
    halo,
    live_in,
    slots,
    own,
    edge_out,
    edge_in,
    pair_out,
    pair_in,
    cross_out,
    cross_in,
    load_sem,
    halo_send,
    halo_recv,
    edge_send,
    edge_recv,
    pair_send,
    pair_recv,
    cross_send,
    cross_recv,
):
    rows, dim = raw.shape
    blocks = rows // BLOCK
    H = R // 2
    per_range = CL_DEV * R
    f32 = jnp.float32
    m, r = lax.axis_index("mz"), lax.axis_index("rep")
    flat = m * R + r
    h, c = r // 2, r % 2
    has_prev, has_next = flat > 0, flat < M * R - 1
    prev = ((flat - 1) // R, (flat + R - 1) % R)
    after = ((flat + 1) // R, (flat + 1) % R)
    partner = (m, 2 * h + 1 - c)
    first, last = r == 0, r == R - 1
    lower, upper = m > 0, m < M - 1
    sends_edge = jnp.logical_or(jnp.logical_and(first, lower), jnp.logical_and(last, upper))
    edge_mz = jnp.where(first, m - 1, m + 1)
    edge_slot = jnp.where(first, 0, 1)

    def load(i):
        at = pl.ds(pl.multiple_of(i * BLOCK, BLOCK), BLOCK)
        return pltpu.make_async_copy(x_hbm.at[at], raw.at[at], load_sem.at[i])

    barrier = pltpu.get_barrier_semaphore()

    def greet(device):
        pl.semaphore_signal(barrier, inc=1, device_id=device, device_id_type=MESH)

    greet(partner)
    for j in range(1, H):
        greet((m, 2 * ((h + j) % H) + c))

    @pl.when(has_prev)
    def _():
        greet(prev)

    @pl.when(has_next)
    def _():
        greet(after)

    @pl.when(sends_edge)
    def _():
        for k in range(R):
            greet((edge_mz, k))

    @pl.when(upper)
    def _():
        greet((m + 1, 0))

    @pl.when(lower)
    def _():
        greet((m - 1, R - 1))

    for i in range(blocks):
        load(i).start()

    as_int = lambda flag: jnp.where(flag, 1, 0)
    pl.semaphore_wait(
        barrier,
        H
        + as_int(has_prev)
        + as_int(has_next)
        + as_int(upper)
        + as_int(lower)
        + R * as_int(sends_edge),
    )

    tail = pl.ds(rows - BLOCK, BLOCK)
    head = pl.ds(0, BLOCK)
    to_next = [
        remote(x_hbm.at[tail], halo.at[0], halo_send.at[0], halo_recv.at[0], after),
        remote(live_ref, live_in.at[0], halo_send.at[1], halo_recv.at[1], after),
    ]
    to_prev = [
        remote(x_hbm.at[head], halo.at[1], halo_send.at[2], halo_recv.at[2], prev),
        remote(live_ref, live_in.at[1], halo_send.at[3], halo_recv.at[3], prev),
    ]

    @pl.when(has_next)
    def _():
        for copy in to_next:
            copy.start()

    @pl.when(has_prev)
    def _():
        for copy in to_prev:
            copy.start()

    def unit(block):
        values = block.astype(f32)
        norm = jnp.sqrt(jnp.sum(values * values, axis=1, keepdims=True) + 1e-06)
        return (values * (1.0 / norm)).astype(jnp.bfloat16)

    live = live_ref[0:1, 0:1]
    position = lax.broadcasted_iota(jnp.int32, (1, rows), 1)
    local = ids_ref[...] - m * per_range
    slot = jnp.where(local < 0, local + 2 * per_range, local)
    slots[...] = jnp.where(position < live, slot, -1)

    def normalise(i, carry):
        load(i).wait()
        at = pl.multiple_of(i * BLOCK, BLOCK)
        ext[pl.ds(at + BLOCK, BLOCK), :] = unit(raw[pl.ds(at, BLOCK), :])
        return carry

    lax.fori_loop(0, blocks, normalise, 0)

    def band(i, low_live, high_live):
        at = pl.multiple_of(i * BLOCK, BLOCK)
        keys = ext[pl.ds(at, 3 * BLOCK), :]
        queries = ext[pl.ds(at + BLOCK, BLOCK), :]
        scores = lax.dot_general(
            queries, keys, (((1,), (1,)), ((), ())), preferred_element_type=f32
        )
        reach = reach_ref[...]
        lane = lax.broadcasted_iota(jnp.int32, reach.shape, 1)
        back = jnp.sum(jnp.where(lane == i, reach, 0.0), axis=1, keepdims=True)
        ahead = jnp.sum(jnp.where(lane == i + blocks, reach, 0.0), axis=1, keepdims=True)
        query = lax.broadcasted_iota(jnp.int32, (BLOCK, 1), 0).astype(f32) + BLOCK
        key_lane = lax.broadcasted_iota(jnp.int32, (1, 3 * BLOCK), 1)
        key_pos = key_lane + (at - BLOCK)
        limit = jnp.where(
            key_pos < 0, low_live - rows, jnp.where(key_pos >= rows, high_live + rows, live)
        )
        key = jnp.where(key_pos < limit, key_lane.astype(f32), f32(-1e6))
        inside = (key >= query - back) & (key <= query + ahead)
        keep = inside | (key_lane.astype(f32) == query)
        weight = jnp.where(keep, jnp.exp(sharpness * (scores - 1.0)), f32(0.0))
        total = jnp.sum(weight, axis=1, keepdims=True)
        mixed = jnp.dot(weight.astype(jnp.bfloat16), keys, preferred_element_type=f32)
        cons[pl.ds(at, BLOCK), :] = (mixed * (1.0 / total)).astype(jnp.bfloat16)

    def inner(i, carry):
        band(i, live, live)
        return carry

    lax.fori_loop(1, blocks - 1, inner, 0)

    @pl.when(has_prev)
    def _():
        for copy in to_next:
            copy.wait_recv()
        ext[0:BLOCK, :] = unit(halo[0])

    @pl.when(jnp.logical_not(has_prev))
    def _():
        ext[0:BLOCK, :] = jnp.zeros((BLOCK, dim), jnp.bfloat16)
        live_in[0] = jnp.zeros(live_in.shape[1:], jnp.int32)

    @pl.when(has_next)
    def _():
        for copy in to_prev:
            copy.wait_recv()
        ext[rows + BLOCK : rows + 2 * BLOCK, :] = unit(halo[1])

    @pl.when(jnp.logical_not(has_next))
    def _():
        ext[rows + BLOCK : rows + 2 * BLOCK, :] = jnp.zeros((BLOCK, dim), jnp.bfloat16)
        live_in[1] = jnp.zeros(live_in.shape[1:], jnp.int32)

    low_live, high_live = live_in[0][0:1, 0:1], live_in[1][0:1, 0:1]

    def outer(j, carry):
        band(j * (blocks - 1), low_live, high_live)
        return carry

    lax.fori_loop(0, 2, outer, 0)

    def partial(base):
        row = lax.broadcasted_iota(jnp.int32, (TILE, rows), 0)
        pick = jnp.where(slots[...] - base == row, f32(1.0), f32(0.0)).astype(jnp.bfloat16)
        return jnp.dot(pick, cons[...], preferred_element_type=f32)

    def each_tile(piece, store):
        def body(t, carry):
            at = pl.multiple_of(t * TILE, TILE)
            store(pl.ds(at, TILE), partial(piece * CL_DEV + at))
            return carry

        lax.fori_loop(0, CL_DEV // TILE, body, 0)

    def edge_copy(j):
        k = (j + jnp.where(first, R // 2, 0)) % R
        return k, remote(
            edge_out.at[j],
            edge_in.at[edge_slot],
            edge_send.at[j],
            edge_recv.at[edge_slot],
            (edge_mz, k),
        )

    @pl.when(sends_edge)
    def _():
        def body(j, carry):
            k, copy = edge_copy(j)

            def store(at, value):
                edge_out[j, at, :] = value.astype(jnp.bfloat16)

            each_tile(R + k, store)
            copy.start()
            return carry

        lax.fori_loop(0, R, body, 0)

    def pair_copy(j):
        return remote(
            pair_out.at[j], pair_in.at[j], pair_send.at[j], pair_recv.at[j], partner
        )

    def cross_copy(j):
        return remote(
            cross_out.at[j - 1],
            cross_in.at[j - 1],
            cross_send.at[j - 1],
            cross_recv.at[j - 1],
            (m, 2 * ((h + j) % H) + c),
        )

    def give(j, carry):
        def store(at, value):
            pair_out[j, at, :] = value.astype(jnp.bfloat16)

        each_tile(2 * ((h + j + 1) % H) + 1 - c, store)
        pair_copy(j).start()
        return carry

    lax.fori_loop(0, H, give, 0)

    def keep_own(j, carry):
        def store(at, value):
            own[at, :] = value

        each_tile(2 * ((h + j + 1) % H) + c, store)
        pair_copy(j).wait_recv()

        @pl.when(j < H - 1)
        def _():
            cross_out[j] = (own[...] + pair_in[j].astype(f32)).astype(jnp.bfloat16)
            cross_copy(j + 1).start()

        return carry

    lax.fori_loop(0, H, keep_own, 0)

    own[...] += pair_in[H - 1].astype(f32)
    for j in range(1, H):
        cross_copy(j).wait_recv()
        own[...] += cross_in[j - 1].astype(f32)

    def edge_arrival(side):
        return remote(
            edge_out.at[0], edge_in.at[side], edge_send.at[0], edge_recv.at[side], partner
        )

    @pl.when(upper)
    def _():
        edge_arrival(0).wait_recv()
        own[...] += edge_in[0].astype(f32)

    @pl.when(lower)
    def _():
        edge_arrival(1).wait_recv()
        own[...] += edge_in[1].astype(f32)

    owned = own[...]
    scale = jnp.sqrt(jnp.mean(owned * owned, axis=1, keepdims=True) + 1e-06)
    out_ref[...] = owned * (1.0 / scale)

    @pl.when(has_next)
    def _():
        for copy in to_next:
            copy.wait_send()

    @pl.when(has_prev)
    def _():
        for copy in to_prev:
            copy.wait_send()

    @pl.when(sends_edge)
    def _():
        for j in range(R):
            edge_copy(j)[1].wait_send()

    for j in range(H):
        pair_copy(j).wait_send()
    for j in range(1, H):
        cross_copy(j).wait_send()


def shards(spectra, reach_back, reach_ahead, live, cluster_ids):
    rows, dim = spectra.shape
    M, R = lax.axis_size("mz"), lax.axis_size("rep")
    H = R // 2
    blocks = rows // BLOCK
    reach = jnp.concatenate(
        [reach_back.reshape(blocks, BLOCK), reach_ahead.reshape(blocks, BLOCK)], axis=0
    )
    reach = reach.astype(jnp.float32).T
    piece = (CL_DEV, dim)
    half = jnp.bfloat16
    dma = pltpu.SemaphoreType.DMA
    vmem = pl.BlockSpec(memory_space=pltpu.VMEM)
    return pl.pallas_call(
        functools.partial(kernel, M, R),
        out_shape=jax.ShapeDtypeStruct((CL_DEV, dim), jnp.float32),
        in_specs=[pl.BlockSpec(memory_space=pl.ANY), vmem, vmem, vmem],
        out_specs=vmem,
        scratch_shapes=[
            pltpu.VMEM((rows, dim), half),
            pltpu.VMEM((rows + 2 * BLOCK, dim), half),
            pltpu.VMEM((rows, dim), half),
            pltpu.VMEM((2, BLOCK, dim), half),
            pltpu.VMEM((2, 8, 128), jnp.int32),
            pltpu.VMEM((1, rows), jnp.int32),
            pltpu.VMEM(piece, jnp.float32),
            pltpu.VMEM((R,) + piece, half),
            pltpu.VMEM((2,) + piece, half),
            pltpu.VMEM((H,) + piece, half),
            pltpu.VMEM((H,) + piece, half),
            pltpu.VMEM((max(H - 1, 1),) + piece, half),
            pltpu.VMEM((max(H - 1, 1),) + piece, half),
            dma((blocks,)),
            dma((4,)),
            dma((4,)),
            dma((R,)),
            dma((2,)),
            dma((H,)),
            dma((H,)),
            dma((max(H - 1, 1),)),
            dma((max(H - 1, 1),)),
        ],
        compiler_params=pltpu.CompilerParams(
            collective_id=0, has_side_effects=True, vmem_limit_bytes=56 * 1024 * 1024
        ),
        name="consensus",
    )(
        spectra,
        reach,
        jnp.broadcast_to(live.reshape(1, 1), (8, 128)),
        cluster_ids.reshape(1, rows),
    )


def solution(mesh):
    return jax.shard_map(
        shards,
        mesh=mesh,
        in_specs=(
            P(("mz", "rep"), None),
            P(("mz", "rep")),
            P(("mz", "rep")),
            P(("mz", "rep")),
            P(("mz", "rep")),
        ),
        out_specs=P(("mz", "rep"), None),
        check_vma=False,
    )
```

```python
import functools

import jax
import jax.numpy as jnp
from jax import lax
from jax.experimental import pallas as pl
from jax.experimental.pallas import tpu as pltpu
from jax.sharding import PartitionSpec as P

BLOCK = 256
CL_DEV = 512
TILE = 256
LANES = 128
MESH = pl.DeviceIdType.MESH

sharpness = 3.0


def remote(src, dst, send_sem, recv_sem, device):
    return pltpu.make_async_remote_copy(
        src_ref=src,
        dst_ref=dst,
        send_sem=send_sem,
        recv_sem=recv_sem,
        device_id=device,
        device_id_type=MESH,
    )


def kernel(
    M,
    R,
    x_hbm,
    back_ref,
    ahead_ref,
    live_ref,
    ids_ref,
    out_ref,
    raw,
    ext,
    cons,
    halo,
    live_out,
    live_in,
    reach_t,
    slots,
    own,
    edge_out,
    edge_in,
    pair_out,
    pair_in,
    cross_out,
    cross_in,
    load_sem,
    halo_send,
    halo_recv,
    edge_send,
    edge_recv,
    pair_send,
    pair_recv,
    cross_send,
    cross_recv,
):
    rows, dim = raw.shape
    blocks = rows // BLOCK
    H = R // 2
    per_range = CL_DEV * R
    f32 = jnp.float32
    m, r = lax.axis_index("mz"), lax.axis_index("rep")
    flat = m * R + r
    h, c = r // 2, r % 2
    has_prev, has_next = flat > 0, flat < M * R - 1
    prev = ((flat - 1) // R, (flat + R - 1) % R)
    after = ((flat + 1) // R, (flat + 1) % R)
    partner = (m, 2 * h + 1 - c)
    first, last = r == 0, r == R - 1
    lower, upper = m > 0, m < M - 1
    sends_edge = jnp.logical_or(jnp.logical_and(first, lower), jnp.logical_and(last, upper))
    edge_mz = jnp.where(first, m - 1, m + 1)
    edge_slot = jnp.where(first, 0, 1)

    def load(i):
        at = pl.ds(pl.multiple_of(i * BLOCK, BLOCK), BLOCK)
        return pltpu.make_async_copy(x_hbm.at[at], raw.at[at], load_sem.at[i])

    barrier = pltpu.get_barrier_semaphore()

    def greet(device):
        pl.semaphore_signal(barrier, inc=1, device_id=device, device_id_type=MESH)

    greet(partner)
    for j in range(1, H):
        greet((m, 2 * ((h + j) % H) + c))

    @pl.when(has_prev)
    def _():
        greet(prev)

    @pl.when(has_next)
    def _():
        greet(after)

    @pl.when(sends_edge)
    def _():
        for k in range(R):
            greet((edge_mz, k))

    @pl.when(upper)
    def _():
        greet((m + 1, 0))

    @pl.when(lower)
    def _():
        greet((m - 1, R - 1))

    for i in range(blocks):
        load(i).start()

    live = live_ref[0]
    live_out[...] = jnp.full(live_out.shape, live, jnp.int32)
    as_int = lambda flag: jnp.where(flag, 1, 0)
    pl.semaphore_wait(
        barrier,
        H
        + as_int(has_prev)
        + as_int(has_next)
        + as_int(upper)
        + as_int(lower)
        + R * as_int(sends_edge),
    )

    tail = pl.ds(rows - BLOCK, BLOCK)
    head = pl.ds(0, BLOCK)
    to_next = [
        remote(x_hbm.at[tail], halo.at[0], halo_send.at[0], halo_recv.at[0], after),
        remote(live_out, live_in.at[0], halo_send.at[1], halo_recv.at[1], after),
    ]
    to_prev = [
        remote(x_hbm.at[head], halo.at[1], halo_send.at[2], halo_recv.at[2], prev),
        remote(live_out, live_in.at[1], halo_send.at[3], halo_recv.at[3], prev),
    ]

    @pl.when(has_next)
    def _():
        for copy in to_next:
            copy.start()

    @pl.when(has_prev)
    def _():
        for copy in to_prev:
            copy.start()

    def unit(block):
        values = block.astype(f32)
        norm = jnp.sqrt(jnp.sum(values * values, axis=1, keepdims=True) + 1e-06)
        return (values * (1.0 / norm)).astype(jnp.bfloat16)

    lines, lanes = ids_ref.shape
    reach = jnp.concatenate(
        [
            back_ref[...].astype(f32),
            ahead_ref[...].astype(f32),
            jnp.zeros((lanes - 2 * lines, lanes), f32),
        ],
        axis=0,
    )
    reach_t[...] = reach.T
    position = lax.broadcasted_iota(jnp.int32, (lines, lanes), 0) * lanes
    position = position + lax.broadcasted_iota(jnp.int32, (lines, lanes), 1)
    local = ids_ref[...] - m * per_range
    slot = jnp.where(local < 0, local + 2 * per_range, local)
    slot = jnp.where(position < live, slot, -1)
    for k in range(lines):
        slots[:, k * lanes : (k + 1) * lanes] = slot[k : k + 1, :]

    def normalise(i):
        at = pl.multiple_of(i * BLOCK, BLOCK)
        ext[pl.ds(at + BLOCK, BLOCK), :] = unit(raw[pl.ds(at, BLOCK), :])

    for i in range(4):
        load(i).wait()
        normalise(i)

    def band(i, low_live, high_live):
        at = pl.multiple_of(i * BLOCK, BLOCK)
        keys = ext[pl.ds(at, 3 * BLOCK), :]
        queries = ext[pl.ds(at + BLOCK, BLOCK), :]
        scores = lax.dot_general(
            queries, keys, (((1,), (1,)), ((), ())), preferred_element_type=f32
        )
        table = reach_t[...]
        lane = lax.broadcasted_iota(jnp.int32, table.shape, 1)
        per_block = BLOCK // lanes

        def column(first_line):
            pick = [
                jnp.sum(jnp.where(lane == first_line + k, table, 0.0), axis=1, keepdims=True)
                for k in range(per_block)
            ]
            return jnp.concatenate(pick, axis=0)

        back = column(i * per_block)
        ahead = column(lines + i * per_block)
        query = lax.broadcasted_iota(jnp.int32, (BLOCK, 1), 0).astype(f32) + BLOCK
        key_lane = lax.broadcasted_iota(jnp.int32, (1, 3 * BLOCK), 1)
        key_pos = key_lane + (at - BLOCK)
        limit = jnp.where(
            key_pos < 0, low_live - rows, jnp.where(key_pos >= rows, high_live + rows, live)
        )
        key = jnp.where(key_pos < limit, key_lane.astype(f32), f32(-1e6))
        inside = (key >= query - back) & (key <= query + ahead)
        keep = inside | (key_lane.astype(f32) == query)
        weight = jnp.where(keep, jnp.exp(sharpness * (scores - 1.0)), f32(0.0))
        total = jnp.sum(weight, axis=1, keepdims=True)
        mixed = jnp.dot(weight.astype(jnp.bfloat16), keys, preferred_element_type=f32)
        cons[pl.ds(at, BLOCK), :] = (mixed * (1.0 / total)).astype(jnp.bfloat16)

    def inner(p, carry):
        for k in range(2):
            load(4 + 2 * p + k).wait()
        for k in range(2):
            band(1 + 2 * p + k, live, live)
        for k in range(2):
            normalise(4 + 2 * p + k)
        return carry

    lax.fori_loop(0, (blocks - 4) // 2, inner, 0)
    for i in range(blocks - 3, blocks - 1):
        band(i, live, live)

    @pl.when(has_prev)
    def _():
        for copy in to_next:
            copy.wait_recv()
        ext[0:BLOCK, :] = unit(halo[0])

    @pl.when(jnp.logical_not(has_prev))
    def _():
        ext[0:BLOCK, :] = jnp.zeros((BLOCK, dim), jnp.bfloat16)
        live_in[0] = jnp.zeros(live_in.shape[1:], jnp.int32)

    @pl.when(has_next)
    def _():
        for copy in to_prev:
            copy.wait_recv()
        ext[rows + BLOCK : rows + 2 * BLOCK, :] = unit(halo[1])

    @pl.when(jnp.logical_not(has_next))
    def _():
        ext[rows + BLOCK : rows + 2 * BLOCK, :] = jnp.zeros((BLOCK, dim), jnp.bfloat16)
        live_in[1] = jnp.zeros(live_in.shape[1:], jnp.int32)

    low_live, high_live = live_in[0][0:1, 0:1], live_in[1][0:1, 0:1]

    band(0, low_live, live)
    band(blocks - 1, live, high_live)

    def partial(base):
        row = lax.broadcasted_iota(jnp.int32, (TILE, rows), 0)
        pick = jnp.where(slots[...] - base == row, f32(1.0), f32(0.0)).astype(jnp.bfloat16)
        return jnp.dot(pick, cons[...], preferred_element_type=f32)

    tiles = CL_DEV // TILE

    def each_tile(piece, use):
        def body(t, carry):
            at = pl.multiple_of(t * TILE, TILE)
            use(t, pl.ds(at, TILE), partial(piece * CL_DEV + at))
            return carry

        lax.fori_loop(0, tiles, body, 0)

    def edge_copy(j, t):
        k = (j + jnp.where(first, R // 2, 0)) % R
        at = pl.ds(pl.multiple_of(t * TILE, TILE), TILE)
        return remote(
            edge_out.at[j, at],
            edge_in.at[edge_slot, at],
            edge_send.at[j, t],
            edge_recv.at[edge_slot, t],
            (edge_mz, k),
        )

    def edges(start, stop):
        @pl.when(sends_edge)
        def _():
            def body(j, carry):
                def use(t, at, value):
                    edge_out[j, at, :] = value.astype(jnp.bfloat16)
                    edge_copy(j, t).start()

                each_tile(R + (j + jnp.where(first, R // 2, 0)) % R, use)
                return carry

            lax.fori_loop(start, stop, body, 0)

    def pair_copy(j, t):
        at = pl.ds(pl.multiple_of(t * TILE, TILE), TILE)
        return remote(
            pair_out.at[j, at],
            pair_in.at[j, at],
            pair_send.at[j, t],
            pair_recv.at[j, t],
            partner,
        )

    def cross_copy(j, t):
        at = pl.ds(pl.multiple_of(t * TILE, TILE), TILE)
        return remote(
            cross_out.at[j, at],
            cross_in.at[j, at],
            cross_send.at[j, t],
            cross_recv.at[j, t],
            (m, 2 * ((h + j + 1) % H) + c),
        )

    def give(j):
        def use(t, at, value):
            pair_out[j, at, :] = value.astype(jnp.bfloat16)
            pair_copy(j, t).start()

        each_tile(2 * ((h + j + 1) % H) + 1 - c, use)

    edges(0, R // 2)
    for j in range(H - 1):
        give(j)

        def forward(t, at, value):
            pair_copy(j, t).wait_recv()
            value = value + pair_in[j, at, :].astype(f32)
            cross_out[j, at, :] = value.astype(jnp.bfloat16)
            cross_copy(j, t).start()

        each_tile(2 * ((h + j + 1) % H) + c, forward)
    edges(R // 2, R)
    give(H - 1)

    def hold(t, at, value):
        own[at, :] = value

    each_tile(2 * h + c, hold)

    for t in range(tiles):
        pair_copy(H - 1, t).wait_recv()
    own[...] += pair_in[H - 1].astype(f32)
    for j in range(H - 1):
        for t in range(tiles):
            cross_copy(j, t).wait_recv()
        own[...] += cross_in[j].astype(f32)

    def edge_arrival(side):
        for t in range(tiles):
            at = pl.ds(t * TILE, TILE)
            remote(
                edge_out.at[0, at],
                edge_in.at[side, at],
                edge_send.at[0, t],
                edge_recv.at[side, t],
                partner,
            ).wait_recv()
        own[...] += edge_in[side].astype(f32)

    @pl.when(upper)
    def _():
        edge_arrival(0)

    @pl.when(lower)
    def _():
        edge_arrival(1)

    owned = own[...]
    scale = jnp.sqrt(jnp.mean(owned * owned, axis=1, keepdims=True) + 1e-06)
    out_ref[...] = owned * (1.0 / scale)

    @pl.when(has_next)
    def _():
        for copy in to_next:
            copy.wait_send()

    @pl.when(has_prev)
    def _():
        for copy in to_prev:
            copy.wait_send()

    @pl.when(sends_edge)
    def _():
        for j in range(R):
            for t in range(tiles):
                edge_copy(j, t).wait_send()

    for t in range(tiles):
        for j in range(H):
            pair_copy(j, t).wait_send()
        for j in range(H - 1):
            cross_copy(j, t).wait_send()


def shards(spectra, reach_back, reach_ahead, live, cluster_ids):
    rows, dim = spectra.shape
    M, R = lax.axis_size("mz"), lax.axis_size("rep")
    H = R // 2
    blocks = rows // BLOCK
    tiles = CL_DEV // TILE
    lines = rows // LANES
    piece = (CL_DEV, dim)
    half = jnp.bfloat16
    dma = pltpu.SemaphoreType.DMA
    vmem = pl.BlockSpec(memory_space=pltpu.VMEM)
    return pl.pallas_call(
        functools.partial(kernel, M, R),
        out_shape=jax.ShapeDtypeStruct((CL_DEV, dim), jnp.float32),
        in_specs=[
            pl.BlockSpec(memory_space=pl.ANY),
            vmem,
            vmem,
            pl.BlockSpec(memory_space=pltpu.SMEM),
            vmem,
        ],
        out_specs=vmem,
        scratch_shapes=[
            pltpu.VMEM((rows, dim), half),
            pltpu.VMEM((rows + 2 * BLOCK, dim), half),
            pltpu.VMEM((rows, dim), half),
            pltpu.VMEM((2, BLOCK, dim), half),
            pltpu.VMEM((8, LANES), jnp.int32),
            pltpu.VMEM((2, 8, LANES), jnp.int32),
            pltpu.VMEM((LANES, LANES), jnp.float32),
            pltpu.VMEM((1, rows), jnp.int32),
            pltpu.VMEM(piece, jnp.float32),
            pltpu.VMEM((R,) + piece, half),
            pltpu.VMEM((2,) + piece, half),
            pltpu.VMEM((H,) + piece, half),
            pltpu.VMEM((H,) + piece, half),
            pltpu.VMEM((max(H - 1, 1),) + piece, half),
            pltpu.VMEM((max(H - 1, 1),) + piece, half),
            dma((blocks,)),
            dma((4,)),
            dma((4,)),
            dma((R, tiles)),
            dma((2, tiles)),
            dma((H, tiles)),
            dma((H, tiles)),
            dma((max(H - 1, 1), tiles)),
            dma((max(H - 1, 1), tiles)),
        ],
        compiler_params=pltpu.CompilerParams(
            collective_id=0, has_side_effects=True, vmem_limit_bytes=56 * 1024 * 1024
        ),
        name="consensus",
    )(
        spectra,
        reach_back.reshape(lines, LANES),
        reach_ahead.reshape(lines, LANES),
        live,
        cluster_ids.reshape(lines, LANES),
    )


def solution(mesh):
    return jax.shard_map(
        shards,
        mesh=mesh,
        in_specs=(
            P(("mz", "rep"), None),
            P(("mz", "rep")),
            P(("mz", "rep")),
            P(("mz", "rep")),
            P(("mz", "rep")),
        ),
        out_specs=P(("mz", "rep"), None),
        check_vma=False,
    )
```

```python
import functools
import math

import jax
import jax.numpy as jnp
from jax import lax
from jax.experimental import pallas as pl
from jax.experimental.pallas import tpu as pltpu
from jax.sharding import PartitionSpec as P

BLOCK = 256
CL_DEV = 512
TILE = 256
LANES = 128
MESH = pl.DeviceIdType.MESH

sharpness = 3.0
rate = sharpness * math.log2(math.e)


def remote(src, dst, send_sem, recv_sem, device):
    return pltpu.make_async_remote_copy(
        src_ref=src,
        dst_ref=dst,
        send_sem=send_sem,
        recv_sem=recv_sem,
        device_id=device,
        device_id_type=MESH,
    )


def kernel(
    M,
    R,
    x_hbm,
    back_ref,
    ahead_ref,
    live_ref,
    ids_ref,
    own,
    raw,
    ext,
    cons,
    halo,
    live_out,
    live_in,
    reach_t,
    slots,
    edge_out,
    edge_in,
    pair_out,
    pair_in,
    cross_out,
    cross_in,
    load_sem,
    halo_send,
    halo_recv,
    edge_send,
    edge_recv,
    pair_send,
    pair_recv,
    cross_send,
    cross_recv,
):
    rows, dim = raw.shape
    blocks = rows // BLOCK
    H = R // 2
    per_range = CL_DEV * R
    f32 = jnp.float32
    m, r = lax.axis_index("mz"), lax.axis_index("rep")
    flat = m * R + r
    h, c = r // 2, r % 2
    has_prev, has_next = flat > 0, flat < M * R - 1
    prev = ((flat - 1) // R, (flat + R - 1) % R)
    after = ((flat + 1) // R, (flat + 1) % R)
    partner = (m, 2 * h + 1 - c)
    first, last = r == 0, r == R - 1
    lower, upper = m > 0, m < M - 1
    sends_edge = jnp.logical_or(jnp.logical_and(first, lower), jnp.logical_and(last, upper))
    edge_mz = jnp.where(first, m - 1, m + 1)
    edge_slot = jnp.where(first, 0, 1)

    def load(i):
        at = pl.ds(pl.multiple_of(i * BLOCK, BLOCK), BLOCK)
        return pltpu.make_async_copy(x_hbm.at[at], raw.at[at], load_sem.at[i])

    barrier = pltpu.get_barrier_semaphore()

    def greet(device):
        pl.semaphore_signal(barrier, inc=1, device_id=device, device_id_type=MESH)

    greet(partner)
    for j in range(1, H):
        greet((m, 2 * ((h + j) % H) + c))

    @pl.when(has_prev)
    def _():
        greet(prev)

    @pl.when(has_next)
    def _():
        greet(after)

    @pl.when(sends_edge)
    def _():
        for k in range(R):
            greet((edge_mz, k))

    @pl.when(upper)
    def _():
        greet((m + 1, 0))

    @pl.when(lower)
    def _():
        greet((m - 1, R - 1))

    for i in range(blocks):
        load(i).start()

    live = live_ref[0]
    live_out[...] = jnp.full(live_out.shape, live, jnp.int32)
    as_int = lambda flag: jnp.where(flag, 1, 0)
    pl.semaphore_wait(
        barrier,
        H
        + as_int(has_prev)
        + as_int(has_next)
        + as_int(upper)
        + as_int(lower)
        + R * as_int(sends_edge),
    )

    tail = pl.ds(rows - BLOCK, BLOCK)
    head = pl.ds(0, BLOCK)
    to_next = [
        remote(x_hbm.at[tail], halo.at[0], halo_send.at[0], halo_recv.at[0], after),
        remote(live_out, live_in.at[0], halo_send.at[1], halo_recv.at[1], after),
    ]
    to_prev = [
        remote(x_hbm.at[head], halo.at[1], halo_send.at[2], halo_recv.at[2], prev),
        remote(live_out, live_in.at[1], halo_send.at[3], halo_recv.at[3], prev),
    ]

    @pl.when(has_next)
    def _():
        for copy in to_next:
            copy.start()

    @pl.when(has_prev)
    def _():
        for copy in to_prev:
            copy.start()

    def unit(block):
        values = block.astype(f32)
        norm = jnp.sqrt(jnp.sum(values * values, axis=1, keepdims=True) + 1e-06)
        return (values * (1.0 / norm)).astype(jnp.bfloat16)

    lines, lanes = ids_ref.shape
    reach = jnp.concatenate(
        [
            back_ref[...].astype(f32),
            ahead_ref[...].astype(f32),
            jnp.zeros((lanes - 2 * lines, lanes), f32),
        ],
        axis=0,
    )
    reach_t[...] = reach.T
    position = lax.broadcasted_iota(jnp.int32, (lines, lanes), 0) * lanes
    position = position + lax.broadcasted_iota(jnp.int32, (lines, lanes), 1)
    local = ids_ref[...] - m * per_range
    slot = jnp.where(local < 0, local + 2 * per_range, local)
    slot = jnp.where(position < live, slot, -1)
    for k in range(lines):
        slots[:, k * lanes : (k + 1) * lanes] = slot[k : k + 1, :]

    def normalise(i):
        at = pl.multiple_of(i * BLOCK, BLOCK)
        ext[pl.ds(at + BLOCK, BLOCK), :] = unit(raw[pl.ds(at, BLOCK), :])

    for i in range(4):
        load(i).wait()
        normalise(i)

    def band(i, low_live, high_live):
        at = pl.multiple_of(i * BLOCK, BLOCK)
        keys = ext[pl.ds(at, 3 * BLOCK), :]
        queries = ext[pl.ds(at + BLOCK, BLOCK), :]
        scores = lax.dot_general(
            queries, keys, (((1,), (1,)), ((), ())), preferred_element_type=f32
        )
        table = reach_t[...]
        lane = lax.broadcasted_iota(jnp.int32, table.shape, 1)
        per_block = BLOCK // lanes

        def column(first_line):
            pick = [
                jnp.sum(jnp.where(lane == first_line + k, table, 0.0), axis=1, keepdims=True)
                for k in range(per_block)
            ]
            return jnp.concatenate(pick, axis=0)

        back = column(i * per_block)
        ahead = column(lines + i * per_block)
        query = lax.broadcasted_iota(jnp.int32, (BLOCK, 1), 0).astype(f32) + BLOCK
        key_lane = lax.broadcasted_iota(jnp.int32, (1, 3 * BLOCK), 1)
        key_pos = key_lane + (at - BLOCK)
        limit = jnp.where(
            key_pos < 0, low_live - rows, jnp.where(key_pos >= rows, high_live + rows, live)
        )
        present = key_pos < limit
        key = key_lane.astype(f32)
        never = f32(1e6)
        key_up = jnp.where(present, key, -never)
        key_down = jnp.where(present, key, never)
        low, high = query - back, query + ahead
        parts = [slice(k * BLOCK, (k + 1) * BLOCK) for k in range(3)]
        middle = (key_up[:, parts[1]] >= low) & (key_up[:, parts[1]] <= high)
        keep = [
            key_up[:, parts[0]] >= low,
            middle | (key[:, parts[1]] == query),
            key_down[:, parts[2]] <= high,
        ]
        weights = [
            jnp.where(keep[k], jnp.exp2((scores[:, parts[k]] - 1.0) * rate), f32(0.0))
            for k in range(3)
        ]
        total = jnp.sum(weights[0] + weights[1] + weights[2], axis=1, keepdims=True)
        weight = jnp.concatenate([w.astype(jnp.bfloat16) for w in weights], axis=1)
        mixed = jnp.dot(weight, keys, preferred_element_type=f32)
        cons[pl.ds(at, BLOCK), :] = (mixed * (1.0 / total)).astype(jnp.bfloat16)

    def inner(p, carry):
        for k in range(2):
            load(4 + 2 * p + k).wait()
        for k in range(2):
            band(1 + 2 * p + k, live, live)
        for k in range(2):
            normalise(4 + 2 * p + k)
        return carry

    lax.fori_loop(0, (blocks - 4) // 2, inner, 0)
    for i in range(blocks - 3, blocks - 1):
        band(i, live, live)

    @pl.when(has_prev)
    def _():
        for copy in to_next:
            copy.wait_recv()
        ext[0:BLOCK, :] = unit(halo[0])

    @pl.when(jnp.logical_not(has_prev))
    def _():
        ext[0:BLOCK, :] = jnp.zeros((BLOCK, dim), jnp.bfloat16)
        live_in[0] = jnp.zeros(live_in.shape[1:], jnp.int32)

    @pl.when(has_next)
    def _():
        for copy in to_prev:
            copy.wait_recv()
        ext[rows + BLOCK : rows + 2 * BLOCK, :] = unit(halo[1])

    @pl.when(jnp.logical_not(has_next))
    def _():
        ext[rows + BLOCK : rows + 2 * BLOCK, :] = jnp.zeros((BLOCK, dim), jnp.bfloat16)
        live_in[1] = jnp.zeros(live_in.shape[1:], jnp.int32)

    low_live, high_live = live_in[0][0:1, 0:1], live_in[1][0:1, 0:1]

    band(0, low_live, live)
    band(blocks - 1, live, high_live)

    def partial(base):
        row = lax.broadcasted_iota(jnp.int32, (TILE, rows), 0)
        pick = jnp.where(slots[...] - base == row, f32(1.0), f32(0.0)).astype(jnp.bfloat16)
        return jnp.dot(pick, cons[...], preferred_element_type=f32)

    tiles = CL_DEV // TILE

    def each_tile(piece, use):
        def body(t, carry):
            at = pl.multiple_of(t * TILE, TILE)
            use(t, pl.ds(at, TILE), partial(piece * CL_DEV + at))
            return carry

        lax.fori_loop(0, tiles, body, 0)

    def edge_copy(j, t):
        k = (j + jnp.where(first, R // 2, 0)) % R
        at = pl.ds(pl.multiple_of(t * TILE, TILE), TILE)
        return remote(
            edge_out.at[j, at],
            edge_in.at[edge_slot, at],
            edge_send.at[j, t],
            edge_recv.at[edge_slot, t],
            (edge_mz, k),
        )

    def edges(start, stop):
        @pl.when(sends_edge)
        def _():
            def body(j, carry):
                def use(t, at, value):
                    edge_out[j, at, :] = value.astype(jnp.bfloat16)
                    edge_copy(j, t).start()

                each_tile(R + (j + jnp.where(first, R // 2, 0)) % R, use)
                return carry

            lax.fori_loop(start, stop, body, 0)

    def pair_copy(j, t):
        at = pl.ds(pl.multiple_of(t * TILE, TILE), TILE)
        return remote(
            pair_out.at[j, at],
            pair_in.at[j, at],
            pair_send.at[j, t],
            pair_recv.at[j, t],
            partner,
        )

    def cross_copy(j, t):
        at = pl.ds(pl.multiple_of(t * TILE, TILE), TILE)
        return remote(
            cross_out.at[j, at],
            cross_in.at[j, at],
            cross_send.at[j, t],
            cross_recv.at[j, t],
            (m, 2 * ((h + j + 1) % H) + c),
        )

    def give(j):
        def use(t, at, value):
            pair_out[j, at, :] = value.astype(jnp.bfloat16)
            pair_copy(j, t).start()

        each_tile(2 * ((h + j + 1) % H) + 1 - c, use)

    edges(0, R // 2)
    for j in range(H - 1):
        give(j)

        def forward(t, at, value):
            pair_copy(j, t).wait_recv()
            value = value + pair_in[j, at, :].astype(f32)
            cross_out[j, at, :] = value.astype(jnp.bfloat16)
            cross_copy(j, t).start()

        each_tile(2 * ((h + j + 1) % H) + c, forward)
    edges(R // 2, R)
    give(H - 1)

    def hold(t, at, value):
        own[at, :] = value

    each_tile(2 * h + c, hold)

    for t in range(tiles):
        pair_copy(H - 1, t).wait_recv()
    own[...] += pair_in[H - 1].astype(f32)
    for j in range(H - 1):
        for t in range(tiles):
            cross_copy(j, t).wait_recv()
        own[...] += cross_in[j].astype(f32)

    def edge_arrival(side):
        for t in range(tiles):
            at = pl.ds(t * TILE, TILE)
            remote(
                edge_out.at[0, at],
                edge_in.at[side, at],
                edge_send.at[0, t],
                edge_recv.at[side, t],
                partner,
            ).wait_recv()
        own[...] += edge_in[side].astype(f32)

    @pl.when(upper)
    def _():
        edge_arrival(0)

    @pl.when(lower)
    def _():
        edge_arrival(1)

    @pl.when(has_next)
    def _():
        for copy in to_next:
            copy.wait_send()

    @pl.when(has_prev)
    def _():
        for copy in to_prev:
            copy.wait_send()

    @pl.when(sends_edge)
    def _():
        for j in range(R):
            for t in range(tiles):
                edge_copy(j, t).wait_send()

    for t in range(tiles):
        for j in range(H):
            pair_copy(j, t).wait_send()
        for j in range(H - 1):
            cross_copy(j, t).wait_send()


def scale_rows(sum_ref, out_ref):
    owned = sum_ref[...]
    scale = jnp.sqrt(jnp.mean(owned * owned, axis=1, keepdims=True) + 1e-06)
    out_ref[...] = owned * (1.0 / scale)


def shards(spectra, reach_back, reach_ahead, live, cluster_ids):
    rows, dim = spectra.shape
    M, R = lax.axis_size("mz"), lax.axis_size("rep")
    H = R // 2
    blocks = rows // BLOCK
    tiles = CL_DEV // TILE
    lines = rows // LANES
    piece = (CL_DEV, dim)
    half = jnp.bfloat16
    dma = pltpu.SemaphoreType.DMA
    vmem = pl.BlockSpec(memory_space=pltpu.VMEM)
    sums = pl.pallas_call(
        functools.partial(kernel, M, R),
        out_shape=jax.ShapeDtypeStruct((CL_DEV, dim), jnp.float32),
        in_specs=[
            pl.BlockSpec(memory_space=pl.ANY),
            vmem,
            vmem,
            pl.BlockSpec(memory_space=pltpu.SMEM),
            vmem,
        ],
        out_specs=vmem,
        scratch_shapes=[
            pltpu.VMEM((rows, dim), half),
            pltpu.VMEM((rows + 2 * BLOCK, dim), half),
            pltpu.VMEM((rows, dim), half),
            pltpu.VMEM((2, BLOCK, dim), half),
            pltpu.VMEM((8, LANES), jnp.int32),
            pltpu.VMEM((2, 8, LANES), jnp.int32),
            pltpu.VMEM((LANES, LANES), jnp.float32),
            pltpu.VMEM((1, rows), jnp.int32),
            pltpu.VMEM((R,) + piece, half),
            pltpu.VMEM((2,) + piece, half),
            pltpu.VMEM((H,) + piece, half),
            pltpu.VMEM((H,) + piece, half),
            pltpu.VMEM((max(H - 1, 1),) + piece, half),
            pltpu.VMEM((max(H - 1, 1),) + piece, half),
            dma((blocks,)),
            dma((4,)),
            dma((4,)),
            dma((R, tiles)),
            dma((2, tiles)),
            dma((H, tiles)),
            dma((H, tiles)),
            dma((max(H - 1, 1), tiles)),
            dma((max(H - 1, 1), tiles)),
        ],
        compiler_params=pltpu.CompilerParams(
            collective_id=0, has_side_effects=True, vmem_limit_bytes=56 * 1024 * 1024
        ),
        name="consensus",
    )(
        spectra,
        reach_back.reshape(lines, LANES),
        reach_ahead.reshape(lines, LANES),
        live,
        cluster_ids.reshape(lines, LANES),
    )
    tile = pl.BlockSpec((TILE, dim), lambda i: (i, 0))
    return pl.pallas_call(
        scale_rows,
        out_shape=jax.ShapeDtypeStruct((CL_DEV, dim), jnp.float32),
        grid=(tiles,),
        in_specs=[tile],
        out_specs=tile,
        name="scale_rows",
    )(sums)


def solution(mesh):
    return jax.shard_map(
        shards,
        mesh=mesh,
        in_specs=(
            P(("mz", "rep"), None),
            P(("mz", "rep")),
            P(("mz", "rep")),
            P(("mz", "rep")),
            P(("mz", "rep")),
        ),
        out_specs=P(("mz", "rep"), None),
        check_vma=False,
    )
```

```python
import functools
import math

import jax
import jax.numpy as jnp
from jax import lax
from jax.experimental import pallas as pl
from jax.experimental.pallas import tpu as pltpu
from jax.sharding import PartitionSpec as P

BLOCK = 256
CL_DEV = 512
TILE = 256
LANES = 128
MESH = pl.DeviceIdType.MESH

sharpness = 3.0
rate = sharpness * math.log2(math.e)


def remote(src, dst, send_sem, recv_sem, device):
    return pltpu.make_async_remote_copy(
        src_ref=src,
        dst_ref=dst,
        send_sem=send_sem,
        recv_sem=recv_sem,
        device_id=device,
        device_id_type=MESH,
    )


def kernel(
    M,
    R,
    x_hbm,
    back_ref,
    ahead_ref,
    live_ref,
    ids_ref,
    own,
    raw,
    ext,
    cons,
    halo,
    live_out,
    live_in,
    reach_t,
    slots,
    edge_out,
    edge_in,
    pair_out,
    pair_in,
    cross_out,
    cross_in,
    load_sem,
    halo_send,
    halo_recv,
    edge_send,
    edge_recv,
    pair_send,
    pair_recv,
    cross_send,
    cross_recv,
):
    rows, dim = raw.shape
    blocks = rows // BLOCK
    H = R // 2
    per_range = CL_DEV * R
    f32 = jnp.float32
    m, r = lax.axis_index("mz"), lax.axis_index("rep")
    flat = m * R + r
    h, c = r // 2, r % 2
    has_prev, has_next = flat > 0, flat < M * R - 1
    prev = ((flat - 1) // R, (flat + R - 1) % R)
    after = ((flat + 1) // R, (flat + 1) % R)
    partner = (m, 2 * h + 1 - c)
    first, last = r == 0, r == R - 1
    lower, upper = m > 0, m < M - 1
    sends_edge = jnp.logical_or(jnp.logical_and(first, lower), jnp.logical_and(last, upper))
    edge_mz = jnp.where(first, m - 1, m + 1)
    edge_slot = jnp.where(first, 0, 1)

    def load(i):
        at = pl.ds(pl.multiple_of(i * BLOCK, BLOCK), BLOCK)
        return pltpu.make_async_copy(x_hbm.at[at], raw.at[at], load_sem.at[i])

    barrier = pltpu.get_barrier_semaphore()

    def greet(device):
        pl.semaphore_signal(barrier, inc=1, device_id=device, device_id_type=MESH)

    greet(partner)
    for j in range(1, H):
        greet((m, 2 * ((h + j) % H) + c))

    @pl.when(has_prev)
    def _():
        greet(prev)

    @pl.when(has_next)
    def _():
        greet(after)

    @pl.when(sends_edge)
    def _():
        for k in range(R):
            greet((edge_mz, k))

    @pl.when(upper)
    def _():
        greet((m + 1, 0))

    @pl.when(lower)
    def _():
        greet((m - 1, R - 1))

    for i in range(blocks):
        load(i).start()

    live = live_ref[0]
    live_out[...] = jnp.full(live_out.shape, live, jnp.int32)
    as_int = lambda flag: jnp.where(flag, 1, 0)
    pl.semaphore_wait(
        barrier,
        H
        + as_int(has_prev)
        + as_int(has_next)
        + as_int(upper)
        + as_int(lower)
        + R * as_int(sends_edge),
    )

    tail = pl.ds(rows - BLOCK, BLOCK)
    head = pl.ds(0, BLOCK)
    to_next = [
        remote(x_hbm.at[tail], halo.at[0], halo_send.at[0], halo_recv.at[0], after),
        remote(live_out, live_in.at[0], halo_send.at[1], halo_recv.at[1], after),
    ]
    to_prev = [
        remote(x_hbm.at[head], halo.at[1], halo_send.at[2], halo_recv.at[2], prev),
        remote(live_out, live_in.at[1], halo_send.at[3], halo_recv.at[3], prev),
    ]

    @pl.when(has_next)
    def _():
        for copy in to_next:
            copy.start()

    @pl.when(has_prev)
    def _():
        for copy in to_prev:
            copy.start()

    def unit(block):
        values = block.astype(f32)
        norm = jnp.sqrt(jnp.sum(values * values, axis=1, keepdims=True) + 1e-06)
        return (values * (1.0 / norm)).astype(jnp.bfloat16)

    lines, lanes = ids_ref.shape
    reach = jnp.concatenate(
        [
            back_ref[...].astype(f32),
            ahead_ref[...].astype(f32),
            jnp.zeros((lanes - 2 * lines, lanes), f32),
        ],
        axis=0,
    )
    reach_t[...] = reach.T
    position = lax.broadcasted_iota(jnp.int32, (lines, lanes), 0) * lanes
    position = position + lax.broadcasted_iota(jnp.int32, (lines, lanes), 1)
    local = ids_ref[...] - m * per_range
    slot = jnp.where(local < 0, local + 2 * per_range, local)
    slot = jnp.where(position < live, slot, -1)
    for k in range(lines):
        slots[:, k * lanes : (k + 1) * lanes] = slot[k : k + 1, :]

    def normalise(i):
        at = pl.multiple_of(i * BLOCK, BLOCK)
        ext[pl.ds(at + BLOCK, BLOCK), :] = unit(raw[pl.ds(at, BLOCK), :])

    for i in range(4):
        load(i).wait()
        normalise(i)

    def band(i, low_live, high_live):
        at = pl.multiple_of(i * BLOCK, BLOCK)
        keys = ext[pl.ds(at, 3 * BLOCK), :]
        queries = ext[pl.ds(at + BLOCK, BLOCK), :]
        scores = lax.dot_general(
            queries, keys, (((1,), (1,)), ((), ())), preferred_element_type=f32
        )
        table = reach_t[...]
        lane = lax.broadcasted_iota(jnp.int32, table.shape, 1)
        per_block = BLOCK // lanes

        def column(first_line):
            pick = [
                jnp.sum(jnp.where(lane == first_line + k, table, 0.0), axis=1, keepdims=True)
                for k in range(per_block)
            ]
            return jnp.concatenate(pick, axis=0)

        back = column(i * per_block)
        ahead = column(lines + i * per_block)
        query = lax.broadcasted_iota(jnp.int32, (BLOCK, 1), 0).astype(f32) + BLOCK
        key_lane = lax.broadcasted_iota(jnp.int32, (1, 3 * BLOCK), 1)
        key_pos = key_lane + (at - BLOCK)
        limit = jnp.where(
            key_pos < 0, low_live - rows, jnp.where(key_pos >= rows, high_live + rows, live)
        )
        present = key_pos < limit
        key = key_lane.astype(f32)
        never = f32(1e6)
        key_up = jnp.where(present, key, -never)
        key_down = jnp.where(present, key, never)
        low, high = query - back, query + ahead
        parts = [slice(k * BLOCK, (k + 1) * BLOCK) for k in range(3)]
        middle = (key_up[:, parts[1]] >= low) & (key_up[:, parts[1]] <= high)
        keep = [
            key_up[:, parts[0]] >= low,
            middle | (key[:, parts[1]] == query),
            key_down[:, parts[2]] <= high,
        ]
        weights = [
            jnp.where(keep[k], jnp.exp2((scores[:, parts[k]] - 1.0) * rate), f32(0.0))
            for k in range(3)
        ]
        total = jnp.sum(weights[0] + weights[1] + weights[2], axis=1, keepdims=True)
        weight = jnp.concatenate([w.astype(jnp.bfloat16) for w in weights], axis=1)
        mixed = jnp.dot(weight, keys, preferred_element_type=f32)
        cons[pl.ds(at, BLOCK), :] = (mixed * (1.0 / total)).astype(jnp.bfloat16)

    def inner(p, carry):
        for k in range(2):
            load(4 + 2 * p + k).wait()
        for k in range(2):
            band(1 + 2 * p + k, live, live)
        for k in range(2):
            normalise(4 + 2 * p + k)
        return carry

    lax.fori_loop(0, (blocks - 4) // 2, inner, 0)
    for i in range(blocks - 3, blocks - 1):
        band(i, live, live)

    @pl.when(has_prev)
    def _():
        for copy in to_next:
            copy.wait_recv()
        ext[0:BLOCK, :] = unit(halo[0])

    @pl.when(jnp.logical_not(has_prev))
    def _():
        ext[0:BLOCK, :] = jnp.zeros((BLOCK, dim), jnp.bfloat16)
        live_in[0] = jnp.zeros(live_in.shape[1:], jnp.int32)

    @pl.when(has_next)
    def _():
        for copy in to_prev:
            copy.wait_recv()
        ext[rows + BLOCK : rows + 2 * BLOCK, :] = unit(halo[1])

    @pl.when(jnp.logical_not(has_next))
    def _():
        ext[rows + BLOCK : rows + 2 * BLOCK, :] = jnp.zeros((BLOCK, dim), jnp.bfloat16)
        live_in[1] = jnp.zeros(live_in.shape[1:], jnp.int32)

    low_live, high_live = live_in[0][0:1, 0:1], live_in[1][0:1, 0:1]

    band(0, low_live, live)
    band(blocks - 1, live, high_live)

    def partial(base):
        row = lax.broadcasted_iota(jnp.int32, (TILE, rows), 0)
        pick = jnp.where(slots[...] - base == row, f32(1.0), f32(0.0)).astype(jnp.bfloat16)
        return jnp.dot(pick, cons[...], preferred_element_type=f32)

    tiles = CL_DEV // TILE

    def each_tile(piece, use):
        def body(t, carry):
            at = pl.multiple_of(t * TILE, TILE)
            use(t, pl.ds(at, TILE), partial(piece * CL_DEV + at))
            return carry

        lax.fori_loop(0, tiles, body, 0)

    def edge_copy(j, t):
        k = (j + jnp.where(first, R // 2, 0)) % R
        at = pl.ds(pl.multiple_of(t * TILE, TILE), TILE)
        return remote(
            edge_out.at[j, at],
            edge_in.at[edge_slot, at],
            edge_send.at[j, t],
            edge_recv.at[edge_slot, t],
            (edge_mz, k),
        )

    def edges(start, stop):
        @pl.when(sends_edge)
        def _():
            def body(j, carry):
                def use(t, at, value):
                    edge_out[j, at, :] = value.astype(jnp.bfloat16)
                    edge_copy(j, t).start()

                each_tile(R + (j + jnp.where(first, R // 2, 0)) % R, use)
                return carry

            lax.fori_loop(start, stop, body, 0)

    def pair_copy(j, t):
        at = pl.ds(pl.multiple_of(t * TILE, TILE), TILE)
        return remote(
            pair_out.at[j, at],
            pair_in.at[j, at],
            pair_send.at[j, t],
            pair_recv.at[j, t],
            partner,
        )

    def cross_copy(j, t):
        at = pl.ds(pl.multiple_of(t * TILE, TILE), TILE)
        return remote(
            cross_out.at[j, at],
            cross_in.at[j, at],
            cross_send.at[j, t],
            cross_recv.at[j, t],
            (m, 2 * ((h + j + 1) % H) + c),
        )

    def give(j):
        def use(t, at, value):
            pair_out[j, at, :] = value.astype(jnp.bfloat16)
            pair_copy(j, t).start()

        each_tile(2 * ((h + j + 1) % H) + 1 - c, use)

    edges(0, 1)
    for j in range(H - 1):
        give(j)

        def forward(t, at, value):
            pair_copy(j, t).wait_recv()
            value = value + pair_in[j, at, :].astype(f32)
            cross_out[j, at, :] = value.astype(jnp.bfloat16)
            cross_copy(j, t).start()

        each_tile(2 * ((h + j + 1) % H) + c, forward)
    edges(1, R)
    give(H - 1)

    def hold(t, at, value):
        own[at, :] = value

    each_tile(2 * h + c, hold)

    for t in range(tiles):
        pair_copy(H - 1, t).wait_recv()
    own[...] += pair_in[H - 1].astype(f32)
    for j in range(H - 1):
        for t in range(tiles):
            cross_copy(j, t).wait_recv()
        own[...] += cross_in[j].astype(f32)

    def edge_arrival(side):
        for t in range(tiles):
            at = pl.ds(t * TILE, TILE)
            remote(
                edge_out.at[0, at],
                edge_in.at[side, at],
                edge_send.at[0, t],
                edge_recv.at[side, t],
                partner,
            ).wait_recv()
        own[...] += edge_in[side].astype(f32)

    @pl.when(upper)
    def _():
        edge_arrival(0)

    @pl.when(lower)
    def _():
        edge_arrival(1)

    @pl.when(has_next)
    def _():
        for copy in to_next:
            copy.wait_send()

    @pl.when(has_prev)
    def _():
        for copy in to_prev:
            copy.wait_send()

    @pl.when(sends_edge)
    def _():
        for j in range(R):
            for t in range(tiles):
                edge_copy(j, t).wait_send()

    for t in range(tiles):
        for j in range(H):
            pair_copy(j, t).wait_send()
        for j in range(H - 1):
            cross_copy(j, t).wait_send()


def scale_rows(sum_ref, out_ref):
    owned = sum_ref[...]
    scale = jnp.sqrt(jnp.mean(owned * owned, axis=1, keepdims=True) + 1e-06)
    out_ref[...] = owned * (1.0 / scale)


def shards(spectra, reach_back, reach_ahead, live, cluster_ids):
    rows, dim = spectra.shape
    M, R = lax.axis_size("mz"), lax.axis_size("rep")
    H = R // 2
    blocks = rows // BLOCK
    tiles = CL_DEV // TILE
    lines = rows // LANES
    piece = (CL_DEV, dim)
    half = jnp.bfloat16
    dma = pltpu.SemaphoreType.DMA
    vmem = pl.BlockSpec(memory_space=pltpu.VMEM)
    sums = pl.pallas_call(
        functools.partial(kernel, M, R),
        out_shape=jax.ShapeDtypeStruct((CL_DEV, dim), jnp.float32),
        in_specs=[
            pl.BlockSpec(memory_space=pl.ANY),
            vmem,
            vmem,
            pl.BlockSpec(memory_space=pltpu.SMEM),
            vmem,
        ],
        out_specs=vmem,
        scratch_shapes=[
            pltpu.VMEM((rows, dim), half),
            pltpu.VMEM((rows + 2 * BLOCK, dim), half),
            pltpu.VMEM((rows, dim), half),
            pltpu.VMEM((2, BLOCK, dim), half),
            pltpu.VMEM((8, LANES), jnp.int32),
            pltpu.VMEM((2, 8, LANES), jnp.int32),
            pltpu.VMEM((LANES, LANES), jnp.float32),
            pltpu.VMEM((1, rows), jnp.int32),
            pltpu.VMEM((R,) + piece, half),
            pltpu.VMEM((2,) + piece, half),
            pltpu.VMEM((H,) + piece, half),
            pltpu.VMEM((H,) + piece, half),
            pltpu.VMEM((max(H - 1, 1),) + piece, half),
            pltpu.VMEM((max(H - 1, 1),) + piece, half),
            dma((blocks,)),
            dma((4,)),
            dma((4,)),
            dma((R, tiles)),
            dma((2, tiles)),
            dma((H, tiles)),
            dma((H, tiles)),
            dma((max(H - 1, 1), tiles)),
            dma((max(H - 1, 1), tiles)),
        ],
        compiler_params=pltpu.CompilerParams(
            collective_id=0, has_side_effects=True, vmem_limit_bytes=56 * 1024 * 1024
        ),
        name="consensus",
    )(
        spectra,
        reach_back.reshape(lines, LANES),
        reach_ahead.reshape(lines, LANES),
        live,
        cluster_ids.reshape(lines, LANES),
    )
    tile = pl.BlockSpec((TILE, dim), lambda i: (i, 0))
    return pl.pallas_call(
        scale_rows,
        out_shape=jax.ShapeDtypeStruct((CL_DEV, dim), jnp.float32),
        grid=(tiles,),
        in_specs=[tile],
        out_specs=tile,
        name="scale_rows",
    )(sums)


def solution(mesh):
    return jax.shard_map(
        shards,
        mesh=mesh,
        in_specs=(
            P(("mz", "rep"), None),
            P(("mz", "rep")),
            P(("mz", "rep")),
            P(("mz", "rep")),
            P(("mz", "rep")),
        ),
        out_specs=P(("mz", "rep"), None),
        check_vma=False,
    )
```
